32 devices in a mesh: ja: 4 (over x, core), ka: 8 (over z, y).
Axes of the slice: x: 2, y: 2, z: 4, core: 2. Of those that a mesh axis runs over, the one named last changes fastest.
Arguments:
- blocks: bfloat16 [128, 128, 128, 128], P(('ja', 'ka')), may hold values from -6 to 6
- coords: int32 [128, 3], P(('ja', 'ka')), may hold values from 0 to 31, as said below
- live_counts: int32 [32], P(('ja', 'ka')), may hold values from 1 to 4, as said below
- mode2_factor: bfloat16 [4096, 512], P(('ja', 'ka')), may hold values from -0.52734375 to 0.52734375
- mode3_factor: bfloat16 [4096, 512], P(('ka', 'ja')), may hold values from -0.52734375 to 0.52734375
Outputs:
- mttkrp: float32 [512, 512], P(('ja', 'ka'))
The draws below stay inside these ranges and needn't reach their ends.
Inputs may be any that keep to these rules, and one draw needn't show every extreme that they name: `coords`: column 0 lies in 0 to 3 and favours some popular row blocks. The device at index j of ja and k of ka holds slots whose column 1 lies in j * 8 to (j + 1) * 8 - 1 and whose column 2 lies in k * 4 to (k + 1) * 4 - 1. `live_counts`: slots of a device beyond its count are dead; some device in every draw has all 4 slots live.
All inputs are finite; a program needn't handle non-finite values.
Results may differ from the reference program's by a relative error of at most 0.0003.
Values may be sent and summed in bfloat16 or wider, within the bound.
No kernel may reach another device: no remote copies, remote signals or barrier semaphores. Data moves between devices by JAX's collectives and lax.ppermute only.
A program may use at most 64 MiB of HBM per device.

```python
import jax
import jax.numpy as jnp
from jax import lax

BS = 128
R = 512
BLK_DEV = 4
NI = 512
NJ = 4096
NK = 4096
NBLK = 128
N_JA = 4
N_KA = 8
DEVICES = 32


def draw_coords(key, part):
    key_one, key_two, key_three, key_four, key_five = jax.random.split(jax.random.fold_in(key, 11), 5)
    row_blocks = NI // BS
    slot_index = jnp.arange(NBLK, dtype=jnp.int32)
    device = slot_index // BLK_DEV
    column = device // N_KA
    within = device % N_KA
    first = jax.random.randint(key_one, (NBLK,), 0, row_blocks, dtype=jnp.int32)
    second = jax.random.randint(key_two, (NBLK,), 0, row_blocks, dtype=jnp.int32)
    offset = jax.random.randint(key_three, (), 0, row_blocks, dtype=jnp.int32)
    mode1_block = (jnp.minimum(first, second) + offset) % row_blocks
    mode2_block = column * N_KA + jax.random.randint(key_four, (NBLK,), 0, N_KA, dtype=jnp.int32)
    mode3_block = within * N_JA + jax.random.randint(key_five, (NBLK,), 0, N_JA, dtype=jnp.int32)
    first_slot = slot_index == 0
    last_slot = slot_index == (DEVICES - 1) * BLK_DEV
    mode1_block = jnp.where(first_slot, 0, jnp.where(last_slot, row_blocks - 1, mode1_block))
    mode2_block = jnp.where(first_slot, 0, jnp.where(last_slot, DEVICES - 1, mode2_block))
    mode3_block = jnp.where(first_slot, 0, jnp.where(last_slot, DEVICES - 1, mode3_block))
    return jnp.stack([mode1_block, mode2_block, mode3_block], axis=1).astype(jnp.int32)


def draw_live_counts(key, part):
    key_one, key_two = jax.random.split(jax.random.fold_in(key, 23), 2)
    counts = jax.random.randint(key_one, (DEVICES,), 1, BLK_DEV + 1, dtype=jnp.int32)
    fullest = jax.random.randint(key_two, (), 0, DEVICES, dtype=jnp.int32)
    device = jnp.arange(DEVICES, dtype=jnp.int32)
    counts = jnp.where(device == (fullest + 1) % DEVICES, 1, counts)
    return jnp.where(device == fullest, BLK_DEV, counts).astype(jnp.int32)


def steps_of(own_key, extent, shards, smallest, high):
    def one(axis_at, shards_of):
        steps = jax.random.uniform(jax.random.fold_in(jax.random.fold_in(own_key, 6), axis_at), (shards_of,), jnp.float32, smallest / len(shards), high / len(shards))
        return jnp.repeat(jnp.exp(steps), extent[axis_at] // shards_of).reshape((-1,) + (1,) * (len(extent) - axis_at - 1))

    factor_of = one(*shards[0])
    for cut in shards[1:]:
        factor_of = factor_of * one(*cut)
    return factor_of


def centred(rng, dims, deviation, most, shards=(), kind=jnp.bfloat16):
    loudness = steps_of(rng, dims, shards, -0.22, 0.18) if shards else 1.0
    values = jax.random.normal(rng, dims, jnp.float32) * deviation * loudness
    return jnp.minimum(jnp.maximum(values, -most), most).astype(kind)


def setup_inputs(seed: int = 0) -> dict:
    key_list = jax.random.split(jax.random.key(seed), 6)
    blocks = centred(key_list[0], (NBLK, BS, BS, BS), 1.0, 6.0, ((0, 32),))
    coords = draw_coords(jax.random.fold_in(key_list[5], 71), 0)
    live_counts = draw_live_counts(jax.random.fold_in(key_list[5], 71), 0)
    mode2_factor = centred(key_list[3], (NJ, R), (BS ** -0.5), 0.52734375, ((0, 32),))
    mode3_factor = centred(key_list[4], (NK, R), (BS ** -0.5), 0.52734375, ((0, 32),))
    return {"blocks": blocks, "coords": coords, "live_counts": live_counts, "mode2_factor": mode2_factor, "mode3_factor": mode3_factor}


def accumulate(totals, block_cube, mode2_rows, mode3_rows, row_start):
    contracted = jnp.einsum("abc,cr->abr", block_cube, mode3_rows, preferred_element_type=jnp.float32)
    block_rows = jnp.einsum("abr,br->ar", contracted, mode2_rows.astype(jnp.float32))
    current = lax.dynamic_slice_in_dim(totals, row_start, block_rows.shape[0], 0)
    return lax.dynamic_update_slice_in_dim(totals, current + block_rows, row_start, 0)


def reference(blocks, coords, live_counts, mode2_factor, mode3_factor):
    block_edge = blocks.shape[1]
    totals = jnp.zeros((NI, R), jnp.float32)

    def add_block(running, slot_index):
        is_live = live_counts[slot_index // BLK_DEV] > slot_index % BLK_DEV

        def apply_block(current):
            position = coords[slot_index]
            block_cube = blocks[slot_index]
            mode2_rows = lax.dynamic_slice_in_dim(mode2_factor, (position[1] * block_edge).astype(jnp.int32), block_edge, 0)
            mode3_rows = lax.dynamic_slice_in_dim(mode3_factor, (position[2] * block_edge).astype(jnp.int32), block_edge, 0)
            return accumulate(current, block_cube, mode2_rows, mode3_rows, (position[0] * block_edge).astype(jnp.int32))

        return lax.cond(is_live, apply_block, lambda current: current, running), None

    totals, _ = lax.scan(add_block, totals, jnp.arange(NBLK, dtype=jnp.int32))
    return totals
```

```python
import functools
import math

import jax
import jax.numpy as jnp
from jax import lax
from jax.experimental import pallas as pl
from jax.experimental.pallas import tpu as pltpu
from jax.sharding import PartitionSpec as P

IROWS_DEV = 16
STEP_ROWS = 64
CHUNKS = 2
BOTH = ("ja", "ka")


def exchange(value, axis, size, code):
    return lax.ppermute(value, axis, [(i, i ^ code) for i in range(size)])


def split_of(size):
    inner = 1
    while inner * inner * 4 <= size:
        inner *= 2
    return inner, size // inner


def far_pieces(own, axis, size):
    inner, outer = split_of(size)
    return [own] + [exchange(own, axis, size, far * inner) for far in range(1, outer)]


def all_pieces(far, axis, size):
    inner, outer = split_of(size)
    pieces = []
    for piece in far:
        pieces += [piece] + [exchange(piece, axis, size, near) for near in range(1, inner)]
    return pieces


def product_kernel(n_ja, n_ka, coords, live, place, x_ref, *refs):
    mode2_refs, mode3_refs = refs[:n_ka], refs[n_ka : n_ka + n_ja]
    kept_ref, sent_ref, total, mode2, mode3 = refs[n_ka + n_ja :]
    slot = pl.program_id(0)
    step = pl.program_id(1)
    rows, edge = x_ref.shape[1:3]
    pieces = rows // IROWS_DEV

    @pl.when((slot == 0) & (step == 0))
    def _():
        total[...] = jnp.zeros_like(total)

    @pl.when(slot < live[0])
    def _():
        @pl.when(step == 0)
        def _():
            mode2_code = lax.rem(coords[slot, 1], n_ka) ^ place[1]
            mode3_code = lax.rem(coords[slot, 2], n_ja) ^ place[0]
            for code, ref in enumerate(mode2_refs):

                @pl.when(mode2_code == code)
                def _(ref=ref):
                    mode2[...] = ref[...].astype(jnp.float32)

            for code, ref in enumerate(mode3_refs):

                @pl.when(mode3_code == code)
                def _(ref=ref):
                    mode3[...] = ref[...]

        width = total.shape[-1]
        cube = x_ref[0].reshape(rows * edge, edge)
        part = jnp.dot(cube, mode3[...], preferred_element_type=jnp.float32)
        part = (part.reshape(rows, edge, width) * mode2[...][None]).sum(axis=1)
        first = (coords[slot, 0] * edge + step * rows) // IROWS_DEV
        for piece in range(pieces):
            code = (first + piece) ^ (place[0] * n_ka + place[1])
            other_core = (code // n_ka) % 2
            order = code // (2 * n_ka) * n_ka + code % n_ka
            total[other_core, order] += part[piece * IROWS_DEV : (piece + 1) * IROWS_DEV]

    @pl.when((slot == pl.num_programs(0) - 1) & (step == pl.num_programs(1) - 1))
    def _():
        kept_ref[...] = total[0]
        sent_ref[...] = total[1]


def products(chunk, n_ja, n_ka, blocks, coords, live_counts, place, mode2_pieces, mode3_pieces):
    slots, edge = blocks.shape[:2]
    rank = mode2_pieces[0].shape[1]
    width = mode2_pieces[-1].shape[1]
    steps = edge // STEP_ROWS
    half = n_ja * n_ka // 2
    half_shape = (half, IROWS_DEV, width)

    def block_at(slot, step, coords, live, place):
        held = slot < live[0]
        return (
            jnp.where(held, slot, live[0] - 1),
            jnp.where(held, step, steps - 1),
            0,
            0,
        )

    def panel_spec(piece):
        if piece.shape[1] == width:
            return pl.BlockSpec((edge, width), lambda *_: (0, 0))
        return pl.BlockSpec((edge, width), lambda *_: (0, chunk))

    half_spec = pl.BlockSpec(half_shape, lambda *_: (0, 0, 0))
    panels = list(mode2_pieces) + list(mode3_pieces)
    flops = 2 * slots * edge**3 * width
    return pl.pallas_call(
        functools.partial(product_kernel, n_ja, n_ka),
        out_shape=[jax.ShapeDtypeStruct(half_shape, jnp.float32)] * 2,
        grid_spec=pltpu.PrefetchScalarGridSpec(
            num_scalar_prefetch=3,
            grid=(slots, steps),
            in_specs=[pl.BlockSpec((1, STEP_ROWS, edge, edge), block_at)]
            + [panel_spec(piece) for piece in panels],
            out_specs=[half_spec] * 2,
            scratch_shapes=[
                pltpu.VMEM((2,) + half_shape, jnp.float32),
                pltpu.VMEM((edge, width), jnp.float32),
                pltpu.VMEM((edge, width), mode3_pieces[0].dtype),
            ],
        ),
        cost_estimate=pl.CostEstimate(
            flops=flops, bytes_accessed=2 * blocks.size, transcendentals=0
        ),
        compiler_params=pltpu.CompilerParams(vmem_limit_bytes=48 << 20),
    )(coords, live_counts, place, blocks, *panels)


def add_kernel(kept_ref, received_ref, *out_refs):
    for order, out_ref in enumerate(out_refs):
        out_ref[...] = kept_ref[order] + received_ref[order]


def add_pieces(kept, received):
    half, rows, width = kept.shape
    return pl.pallas_call(
        add_kernel,
        out_shape=[jax.ShapeDtypeStruct((rows, width), jnp.float32)] * half,
        compiler_params=pltpu.CompilerParams(vmem_limit_bytes=12 << 20),
    )(kept, received)


def sum_kernel(count, *refs):
    out_ref = refs[-1]
    width = refs[0].shape[1]
    for chunk in range((len(refs) - 1) // count):
        total = refs[chunk * count][...]
        for ref in refs[chunk * count + 1 : (chunk + 1) * count]:
            total = total + ref[...]
        out_ref[:, chunk * width : (chunk + 1) * width] = total


def scatter(pieces, devices, n_ka):
    arrived = [pieces[0]]
    for order in range(1, len(pieces)):
        code = order // n_ka * 2 * n_ka + order % n_ka
        arrived.append(exchange(pieces[order], BOTH, devices, code))
    return arrived


def on_device(blocks, coords, live_counts, mode2_factor, mode3_factor):
    n_ja = lax.axis_size("ja")
    n_ka = lax.axis_size("ka")
    devices = n_ja * n_ka
    rank = mode2_factor.shape[1]
    width = rank // CHUNKS
    place = jnp.stack([lax.axis_index("ja"), lax.axis_index("ka")]).astype(jnp.int32)

    mode2_far, mode3_far = [], []
    for chunk in range(CHUNKS):
        cols = slice(chunk * width, (chunk + 1) * width)
        mode2_far.append(far_pieces(mode2_factor[:, cols], "ka", n_ka))
        mode3_far.append(far_pieces(mode3_factor[:, cols], "ja", n_ja))

    arrived = []
    pieces = None
    for chunk in range(CHUNKS):
        mode2_pieces = all_pieces(mode2_far[chunk], "ka", n_ka)
        mode3_pieces = all_pieces(mode3_far[chunk], "ja", n_ja)
        if chunk + 1 < CHUNKS:
            mode2_pieces, mode3_pieces, mode2_far[chunk + 1], mode3_far[chunk + 1] = (
                lax.optimization_barrier(
                    (mode2_pieces, mode3_pieces, mode2_far[chunk + 1], mode3_far[chunk + 1])
                )
            )
        if pieces is not None:
            pieces, mode2_pieces, mode3_pieces = lax.optimization_barrier(
                (pieces, mode2_pieces, mode3_pieces)
            )
            arrived += scatter(pieces, devices, n_ka)
        kept, sent = products(
            chunk, n_ja, n_ka, blocks, coords, live_counts, place, mode2_pieces, mode3_pieces
        )
        received = exchange(sent, BOTH, devices, n_ka)
        pieces = list(add_pieces(kept, received))
    arrived += scatter(pieces, devices, n_ka)
    return pl.pallas_call(
        functools.partial(sum_kernel, devices // 2),
        out_shape=jax.ShapeDtypeStruct((IROWS_DEV, rank), jnp.float32),
        compiler_params=pltpu.CompilerParams(vmem_limit_bytes=12 << 20),
    )(*arrived)


def solution(mesh):
    placed = (
        P(BOTH, None, None, None),
        P(BOTH, None),
        P(BOTH),
        P(BOTH, None),
        P(("ka", "ja"), None),
    )
    return jax.shard_map(
        on_device, mesh=mesh, in_specs=placed, out_specs=P(BOTH, None), check_vma=False
    )
```

```python
import functools

import jax
import jax.numpy as jnp
from jax import lax
from jax.experimental import pallas as pl
from jax.experimental.pallas import tpu as pltpu
from jax.sharding import Mesh
from jax.sharding import PartitionSpec as P

IROWS_DEV = 16
CORES = 2
STEP_ROWS = 64
DOT_COLS = 256
PLACES = ("x", "core", "z", "y")
CHIPS = ("x", "z", "y")


def exchange(value, axis, code):
    size = lax.axis_size(axis)
    return lax.ppermute(value, axis, [(i, i ^ code) for i in range(size)])


def far_then_near(own, far, near):
    columns = [own] + [exchange(own, far, code) for code in range(1, lax.axis_size(far))]
    pieces = []
    for column in columns:
        pieces += [column]
        pieces += [exchange(column, near, code) for code in range(1, lax.axis_size(near))]
    return pieces


def product_kernel(n_ja, n_ka, coords, live, place, x_ref, *refs):
    mode2_refs, mode3_refs = refs[:n_ka], refs[n_ka : n_ka + n_ja]
    kept_ref, sent_ref, total, mode2, mode3 = refs[n_ka + n_ja :]
    slot, step, part_of = (pl.program_id(axis) for axis in range(3))
    rows, edge = x_ref.shape[1:3]
    last = [pl.num_programs(axis) - 1 for axis in range(3)]

    @pl.when((slot == 0) & (step == 0) & (part_of == 0))
    def _():
        total[...] = jnp.zeros_like(total)

    @pl.when(slot < live[0])
    def _():
        @pl.when((step == 0) & (part_of == 0))
        def _():
            mode2_code = lax.rem(coords[slot, 1], n_ka) ^ place[1]
            mode3_code = lax.rem(coords[slot, 2], n_ja) ^ place[0]
            for code, ref in enumerate(mode2_refs):

                @pl.when(mode2_code == code)
                def _(ref=ref):
                    mode2[...] = ref[...].astype(jnp.float32)

            for code, ref in enumerate(mode3_refs):

                @pl.when(mode3_code == code)
                def _(ref=ref):
                    mode3[...] = ref[...]

        cols = pl.ds(pl.multiple_of(part_of * DOT_COLS, DOT_COLS), DOT_COLS)
        cube = x_ref[0].reshape(rows * edge, edge)
        part = jnp.dot(cube, mode3[:, cols], preferred_element_type=jnp.float32)
        part = (part.reshape(rows, edge, DOT_COLS) * mode2[:, cols][None]).sum(axis=1)
        first = (coords[slot, 0] * edge + step * rows) // IROWS_DEV
        for piece in range(rows // IROWS_DEV):
            owner = first + piece
            core = owner // n_ka % CORES
            chip = owner // n_ka // CORES * n_ka + owner % n_ka
            total[core ^ place[2], chip, :, cols] += part[
                piece * IROWS_DEV : (piece + 1) * IROWS_DEV
            ]

    @pl.when((slot == last[0]) & (step == last[1]) & (part_of == last[2]))
    def _():
        kept_ref[...] = total[0]
        sent_ref[...] = total[1]


def products(blocks, coords, live_counts, place, mode2_pieces, mode3_pieces):
    slots, edge = blocks.shape[:2]
    rank = mode2_pieces[0].shape[1]
    n_ka, n_ja = len(mode2_pieces), len(mode3_pieces)
    steps = edge // STEP_ROWS
    half_shape = (n_ja * n_ka // CORES, IROWS_DEV, rank)

    def block_at(slot, step, part_of, coords, live, place):
        held = slot < live[0]
        return (
            jnp.where(held, slot, live[0] - 1),
            jnp.where(held, step, steps - 1),
            0,
            0,
        )

    half_spec = pl.BlockSpec(half_shape, lambda *_: (0, 0, 0))
    panel_spec = pl.BlockSpec((edge, rank), lambda *_: (0, 0))
    panels = mode2_pieces + mode3_pieces
    return pl.pallas_call(
        functools.partial(product_kernel, n_ja, n_ka),
        out_shape=[jax.ShapeDtypeStruct(half_shape, jnp.float32)] * 2,
        grid_spec=pltpu.PrefetchScalarGridSpec(
            num_scalar_prefetch=3,
            grid=(slots, steps, rank // DOT_COLS),
            in_specs=[pl.BlockSpec((1, STEP_ROWS, edge, edge), block_at)]
            + [panel_spec] * len(panels),
            out_specs=[half_spec] * 2,
            scratch_shapes=[
                pltpu.VMEM((CORES,) + half_shape, jnp.float32),
                pltpu.VMEM((edge, rank), jnp.float32),
                pltpu.VMEM((edge, rank), mode3_pieces[0].dtype),
            ],
        ),
        cost_estimate=pl.CostEstimate(
            flops=2 * slots * edge**3 * rank, bytes_accessed=2 * blocks.size, transcendentals=0
        ),
        compiler_params=pltpu.CompilerParams(vmem_limit_bytes=48 << 20),
    )(coords, live_counts, place, blocks, *panels)


def on_device(blocks, coords, live_counts, mode2_factor, mode3_factor):
    x, core, z, y = (lax.axis_index(axis) for axis in PLACES)
    place = jnp.stack([x * CORES + core, z * lax.axis_size("y") + y, core]).astype(jnp.int32)
    mode2_pieces = far_then_near(mode2_factor, "z", "y")
    mode3_pieces = far_then_near(mode3_factor, "x", "core")
    kept, sent = products(blocks, coords, live_counts, place, mode2_pieces, mode3_pieces)
    received = exchange(sent, "core", 1)
    arrived = lax.all_to_all(kept + received, CHIPS, 0, 0, tiled=True)
    return arrived.sum(axis=0)


def solution(mesh):
    n_ja, n_ka = mesh.devices.shape
    near = 1
    while near * near * 4 <= n_ka:
        near *= 2
    places = Mesh(mesh.devices.reshape(n_ja // CORES, CORES, n_ka // near, near), PLACES)
    placed = (
        P(PLACES, None, None, None),
        P(PLACES, None),
        P(PLACES),
        P(PLACES, None),
        P(("z", "y", "x", "core"), None),
    )
    return jax.shard_map(
        on_device, mesh=places, in_specs=placed, out_specs=P(PLACES, None), check_vma=False
    )
```

```python
import functools

import jax
import jax.numpy as jnp
from jax import lax
from jax.experimental import pallas as pl
from jax.experimental.pallas import tpu as pltpu
from jax.sharding import Mesh
from jax.sharding import PartitionSpec as P

IROWS_DEV = 16
CORES = 2
STEP_ROWS = 64
DOT_COLS = 256
PLACES = ("x", "core", "z", "y")
CHIPS = ("x", "z", "y")


def exchange(value, axis, code):
    size = lax.axis_size(axis)
    return lax.ppermute(value, axis, [(i, i ^ code) for i in range(size)])


def far_then_near(own, far, near):
    size = lax.axis_size(far)
    columns = [own] + [exchange(own, far, code) for code in range(1, max(2, size - 1))]
    columns[0], columns[1] = lax.optimization_barrier((own, columns[1]))
    columns += [exchange(columns[0], far, code) for code in range(len(columns), size)]
    pieces = []
    for column in columns:
        pieces += [column]
        pieces += [exchange(column, near, code) for code in range(1, lax.axis_size(near))]
    return pieces


def product_kernel(n_ja, n_ka, table, live, x_ref, *refs):
    mode2_refs, mode3_refs = refs[:n_ka], refs[n_ka : n_ka + n_ja]
    kept_ref, sent_ref, mode2, mode3 = refs[n_ka + n_ja :]
    slot, step, part_of = (pl.program_id(axis) for axis in range(3))
    rows, edge = x_ref.shape[1:3]

    @pl.when((slot == 0) & (step == 0) & (part_of == 0))
    def _():
        kept_ref[...] = jnp.zeros_like(kept_ref)
        sent_ref[...] = jnp.zeros_like(sent_ref)

    @pl.when(slot < live[0])
    def _():
        @pl.when((step == 0) & (part_of == 0))
        def _():
            for code, ref in enumerate(mode2_refs):

                @pl.when(table[slot, 1] == code)
                def _(ref=ref):
                    mode2[...] = ref[...].astype(jnp.float32)

            for code, ref in enumerate(mode3_refs):

                @pl.when(table[slot, 2] == code)
                def _(ref=ref):
                    mode3[...] = ref[...]

        cols = pl.ds(pl.multiple_of(part_of * DOT_COLS, DOT_COLS), DOT_COLS)
        cube = x_ref[0].reshape(rows * edge, edge)
        part = jnp.dot(cube, mode3[:, cols], preferred_element_type=jnp.float32)
        part = (part.reshape(rows, edge, DOT_COLS) * mode2[:, cols][None]).sum(axis=1)
        first = (table[slot, 0] * edge + step * rows) // IROWS_DEV
        column = first // n_ka
        chip = column // CORES * n_ka + first % n_ka

        def add_to(ref):
            for piece in range(rows // IROWS_DEV):
                ref[chip + piece, :, cols] += part[piece * IROWS_DEV : (piece + 1) * IROWS_DEV]

        pl.when(column % CORES == table[slot, 3])(functools.partial(add_to, kept_ref))
        pl.when(column % CORES != table[slot, 3])(functools.partial(add_to, sent_ref))


def products(blocks, table, live_counts, mode2_pieces, mode3_pieces):
    slots, edge = blocks.shape[:2]
    rank = mode2_pieces[0].shape[1]
    n_ka, n_ja = len(mode2_pieces), len(mode3_pieces)
    steps = edge // STEP_ROWS
    half_shape = (n_ja * n_ka // CORES, IROWS_DEV, rank)

    def block_at(slot, step, part_of, table, live):
        held = slot < live[0]
        return (
            jnp.where(held, slot, live[0] - 1),
            jnp.where(held, step, steps - 1),
            0,
            0,
        )

    half_spec = pl.BlockSpec(half_shape, lambda *_: (0, 0, 0))
    panel_spec = pl.BlockSpec((edge, rank), lambda *_: (0, 0))
    panels = mode2_pieces + mode3_pieces
    return pl.pallas_call(
        functools.partial(product_kernel, n_ja, n_ka),
        out_shape=[jax.ShapeDtypeStruct(half_shape, jnp.float32)] * 2,
        grid_spec=pltpu.PrefetchScalarGridSpec(
            num_scalar_prefetch=2,
            grid=(slots, steps, rank // DOT_COLS),
            in_specs=[pl.BlockSpec((1, STEP_ROWS, edge, edge), block_at)]
            + [panel_spec] * len(panels),
            out_specs=[half_spec] * 2,
            scratch_shapes=[
                pltpu.VMEM((edge, rank), jnp.float32),
                pltpu.VMEM((edge, rank), mode3_pieces[0].dtype),
            ],
        ),
        cost_estimate=pl.CostEstimate(
            flops=2 * slots * edge**3 * rank, bytes_accessed=2 * blocks.size, transcendentals=0
        ),
        compiler_params=pltpu.CompilerParams(vmem_limit_bytes=48 << 20),
    )(table, live_counts, blocks, *panels)


def on_device(blocks, coords, live_counts, mode2_factor, mode3_factor):
    x, core, z, y = (lax.axis_index(axis) for axis in PLACES)
    n_ja, n_ka = lax.axis_size(("x", "core")), lax.axis_size(("z", "y"))
    table = jnp.stack(
        [
            coords[:, 0],
            lax.rem(coords[:, 1], n_ka) ^ (z * lax.axis_size("y") + y),
            lax.rem(coords[:, 2], n_ja) ^ (x * CORES + core),
            jnp.broadcast_to(core, coords.shape[:1]),
        ],
        axis=1,
    )
    mode2_pieces = far_then_near(mode2_factor, "z", "y")
    mode3_pieces = far_then_near(mode3_factor, "x", "core")
    mode2_pieces[0] = pltpu.with_memory_space_constraint(mode2_factor, pltpu.HBM)
    mode3_pieces[0] = pltpu.with_memory_space_constraint(mode3_factor, pltpu.HBM)
    kept, sent = products(blocks, table, live_counts, mode2_pieces, mode3_pieces)
    received = exchange(sent, "core", 1)
    arrived = lax.all_to_all(kept + received, CHIPS, 0, 0, tiled=True)
    return arrived.sum(axis=0)


def solution(mesh):
    n_ja, n_ka = mesh.devices.shape
    near = 1
    while near * near * 4 <= n_ka:
        near *= 2
    places = Mesh(mesh.devices.reshape(n_ja // CORES, CORES, n_ka // near, near), PLACES)
    placed = (
        P(PLACES, None, None, None),
        P(PLACES, None),
        P(PLACES),
        P(PLACES, None),
        P(("z", "y", "x", "core"), None),
    )
    return jax.shard_map(
        on_device, mesh=places, in_specs=placed, out_specs=P(PLACES, None), check_vma=False
    )
```

```python
import functools

import jax
import jax.numpy as jnp
from jax import lax
from jax.experimental import pallas as pl
from jax.experimental.pallas import tpu as pltpu
from jax.sharding import Mesh
from jax.sharding import PartitionSpec as P


IROWS_DEV = 16
CORES = 2
STEP_ROWS = 64
DOT_COLS = 256
PLACES = ("x", "core", "z", "y")
CHIPS = ("x", "z", "y")


def exchange(value, axis, code):
    size = lax.axis_size(axis)
    return lax.ppermute(value, axis, [(i, i ^ code) for i in range(size)])


def gather_pieces(own, far, near):
    far_size, near_size = lax.axis_size(far), lax.axis_size(near)
    pieces = {(0, 0): own}

    def fetch(code, source, axis, step):
        pieces[code] = exchange(pieces[source], axis, step)

    for far_code in range(far_size):
        low = far_code & -far_code
        rest = far_code ^ low
        if low and not rest:
            fetch((far_code, 0), (0, 0), far, far_code)
        elif low:
            fetch((far_code, 0), (rest, 0), far, low)
        for near_code in range(1, near_size):
            if rest:
                fetch((far_code, near_code), (low, near_code), far, rest)
            else:
                fetch((far_code, near_code), (far_code, 0), near, near_code)
    return [pieces[code] for code in sorted(pieces)]


def product_kernel(n_ja, n_ka, table, live, x_ref, *refs):
    mode2_refs, mode3_refs = refs[:n_ka], refs[n_ka : n_ka + n_ja]
    kept_ref, sent_ref, mode2, mode3 = refs[n_ka + n_ja :]
    slot, step, part_of = (pl.program_id(axis) for axis in range(3))
    rows, edge = x_ref.shape[1:3]

    @pl.when((slot == 0) & (step == 0) & (part_of == 0))
    def _():
        kept_ref[...] = jnp.zeros_like(kept_ref)
        sent_ref[...] = jnp.zeros_like(sent_ref)

    @pl.when(slot < live[0])
    def _():
        @pl.when((step == 0) & (part_of == 0))
        def _():
            for code, ref in enumerate(mode2_refs):

                @pl.when(table[slot, 1] == code)
                def _(ref=ref):
                    mode2[...] = ref[...].astype(jnp.float32)

            for code, ref in enumerate(mode3_refs):

                @pl.when(table[slot, 2] == code)
                def _(ref=ref):
                    mode3[...] = ref[...]

        cols = pl.ds(pl.multiple_of(part_of * DOT_COLS, DOT_COLS), DOT_COLS)
        cube = x_ref[0].reshape(rows * edge, edge)
        part = jnp.dot(cube, mode3[:, cols], preferred_element_type=jnp.float32)
        part = (part.reshape(rows, edge, DOT_COLS) * mode2[:, cols][None]).sum(axis=1)
        first = (table[slot, 0] * edge + step * rows) // IROWS_DEV
        column = first // n_ka
        chip = column // CORES * n_ka + first % n_ka

        def add_to(ref):
            for piece in range(rows // IROWS_DEV):
                ref[chip + piece, :, cols] += part[piece * IROWS_DEV : (piece + 1) * IROWS_DEV]

        pl.when(column % CORES == table[slot, 3])(functools.partial(add_to, kept_ref))
        pl.when(column % CORES != table[slot, 3])(functools.partial(add_to, sent_ref))


def products(blocks, table, live_counts, mode2_pieces, mode3_pieces):
    slots, edge = blocks.shape[:2]
    rank = mode2_pieces[0].shape[1]
    n_ka, n_ja = len(mode2_pieces), len(mode3_pieces)
    steps = edge // STEP_ROWS
    half_shape = (n_ja * n_ka // CORES, IROWS_DEV, rank)

    def block_at(slot, step, part_of, table, live):
        held = slot < live[0]
        return (
            jnp.where(held, slot, live[0] - 1),
            jnp.where(held, step, steps - 1),
            0,
            0,
        )

    half_spec = pl.BlockSpec(half_shape, lambda *_: (0, 0, 0))
    panel_spec = pl.BlockSpec((edge, rank), lambda *_: (0, 0))
    panels = mode2_pieces + mode3_pieces
    return pl.pallas_call(
        functools.partial(product_kernel, n_ja, n_ka),
        out_shape=[jax.ShapeDtypeStruct(half_shape, jnp.float32)] * 2,
        grid_spec=pltpu.PrefetchScalarGridSpec(
            num_scalar_prefetch=2,
            grid=(slots, steps, rank // DOT_COLS),
            in_specs=[pl.BlockSpec((1, STEP_ROWS, edge, edge), block_at)]
            + [panel_spec] * len(panels),
            out_specs=[half_spec] * 2,
            scratch_shapes=[
                pltpu.VMEM((edge, rank), jnp.float32),
                pltpu.VMEM((edge, rank), mode3_pieces[0].dtype),
            ],
        ),
        cost_estimate=pl.CostEstimate(
            flops=2 * slots * edge**3 * rank, bytes_accessed=2 * blocks.size, transcendentals=0
        ),
        compiler_params=pltpu.CompilerParams(vmem_limit_bytes=48 << 20),
    )(table, live_counts, blocks, *panels)


def on_device(blocks, coords, live_counts, mode2_factor, mode3_factor):
    x, core, z, y = (lax.axis_index(axis) for axis in PLACES)
    n_ja, n_ka = lax.axis_size(("x", "core")), lax.axis_size(("z", "y"))
    table = jnp.stack(
        [
            coords[:, 0],
            lax.rem(coords[:, 1], n_ka) ^ (z * lax.axis_size("y") + y),
            lax.rem(coords[:, 2], n_ja) ^ (x * CORES + core),
            jnp.broadcast_to(core, coords.shape[:1]),
        ],
        axis=1,
    )
    mode2_pieces = gather_pieces(mode2_factor, "z", "y")
    mode3_pieces = gather_pieces(mode3_factor, "x", "core")
    mode2_pieces[0] = pltpu.with_memory_space_constraint(mode2_factor, pltpu.HBM)
    mode3_pieces[0] = pltpu.with_memory_space_constraint(mode3_factor, pltpu.HBM)
    kept, sent = products(blocks, table, live_counts, mode2_pieces, mode3_pieces)
    received = exchange(sent, "core", 1)
    arrived = lax.all_to_all(kept + received, CHIPS, 0, 0, tiled=True)
    return arrived.sum(axis=0)


def solution(mesh):
    n_ja, n_ka = mesh.devices.shape
    near = 1
    while near * near * 4 <= n_ka:
        near *= 2
    places = Mesh(mesh.devices.reshape(n_ja // CORES, CORES, n_ka // near, near), PLACES)
    placed = (
        P(PLACES, None, None, None),
        P(PLACES, None),
        P(PLACES),
        P(PLACES, None),
        P(("z", "y", "x", "core"), None),
    )
    return jax.shard_map(
        on_device, mesh=places, in_specs=placed, out_specs=P(PLACES, None), check_vma=False
    )
```

```python
import functools

import jax
import jax.numpy as jnp
from jax import lax
from jax.experimental import pallas as pl
from jax.experimental.pallas import tpu as pltpu
from jax.sharding import Mesh
from jax.sharding import PartitionSpec as P


IROWS_DEV = 16
CORES = 2
STEP_ROWS = 64
DOT_COLS = 512
PLACES = ("x", "core", "z", "y")
CHIPS = ("x", "z", "y")


def exchange(value, axis, code):
    size = lax.axis_size(axis)
    return lax.ppermute(value, axis, [(i, i ^ code) for i in range(size)])


def gather_pieces(own, far, near):
    far_size, near_size = lax.axis_size(far), lax.axis_size(near)
    pieces = {(0, 0): own}

    def fetch(code, source, axis, step):
        pieces[code] = exchange(pieces[source], axis, step)

    for far_code in range(far_size):
        low = far_code & -far_code
        rest = far_code ^ low
        if low and not rest:
            fetch((far_code, 0), (0, 0), far, far_code)
        elif low:
            fetch((far_code, 0), (rest, 0), far, low)
        for near_code in range(1, near_size):
            if rest:
                fetch((far_code, near_code), (low, near_code), far, rest)
            else:
                fetch((far_code, near_code), (far_code, 0), near, near_code)
    return [pieces[code] for code in sorted(pieces)]


def product_kernel(n_ja, n_ka, table, live, x_ref, *refs):
    mode2_refs, mode3_refs = refs[:n_ka], refs[n_ka : n_ka + n_ja]
    kept_ref, sent_ref, mode2, mode3 = refs[n_ka + n_ja + 2 :]
    slot, step, part_of = (pl.program_id(axis) for axis in range(3))
    rows, edge = x_ref.shape[1:3]

    @pl.when(slot < live[0])
    def _():
        @pl.when((step == 0) & (part_of == 0))
        def _():
            for code, ref in enumerate(mode2_refs):

                @pl.when(table[slot, 1] == code)
                def _(ref=ref):
                    mode2[...] = ref[...].astype(jnp.float32)

            for code, ref in enumerate(mode3_refs):

                @pl.when(table[slot, 2] == code)
                def _(ref=ref):
                    mode3[...] = ref[...]

        cols = pl.ds(pl.multiple_of(part_of * DOT_COLS, DOT_COLS), DOT_COLS)
        cube = x_ref[0].reshape(rows * edge, edge)
        part = jnp.dot(cube, mode3[:, cols], preferred_element_type=jnp.float32)
        part = (part.reshape(rows, edge, DOT_COLS) * mode2[:, cols][None]).sum(axis=1)
        first = (table[slot, 0] * edge + step * rows) // IROWS_DEV
        column = first // n_ka
        chip = column // CORES * n_ka + first % n_ka

        def add_to(ref):
            for piece in range(rows // IROWS_DEV):
                ref[chip + piece, :, cols] += part[piece * IROWS_DEV : (piece + 1) * IROWS_DEV]

        pl.when(column % CORES == table[slot, 3])(functools.partial(add_to, kept_ref))
        pl.when(column % CORES != table[slot, 3])(functools.partial(add_to, sent_ref))


def products(blocks, table, live_counts, mode2_pieces, mode3_pieces):
    slots, edge = blocks.shape[:2]
    rank = mode2_pieces[0].shape[1]
    n_ka, n_ja = len(mode2_pieces), len(mode3_pieces)
    steps = edge // STEP_ROWS
    half_shape = (n_ja * n_ka // CORES, IROWS_DEV, rank)

    def block_at(slot, step, part_of, table, live):
        held = slot < live[0]
        return (
            jnp.where(held, slot, live[0] - 1),
            jnp.where(held, step, steps - 1),
            0,
            0,
        )

    in_place = pl.BlockSpec(memory_space=pltpu.VMEM)
    own_spec = pl.BlockSpec((edge, rank), lambda *_: (0, 0))
    panels = mode2_pieces + mode3_pieces
    empty = jnp.zeros(half_shape, jnp.float32)
    return pl.pallas_call(
        functools.partial(product_kernel, n_ja, n_ka),
        out_shape=[jax.ShapeDtypeStruct(half_shape, jnp.float32)] * 2,
        grid_spec=pltpu.PrefetchScalarGridSpec(
            num_scalar_prefetch=2,
            grid=(slots, steps, rank // DOT_COLS),
            in_specs=[pl.BlockSpec((1, STEP_ROWS, edge, edge), block_at)]
            + ([own_spec] + [in_place] * (n_ka - 1))
            + ([own_spec] + [in_place] * (n_ja - 1))
            + [in_place] * 2,
            out_specs=[in_place] * 2,
            scratch_shapes=[
                pltpu.VMEM((edge, rank), jnp.float32),
                pltpu.VMEM((edge, rank), mode3_pieces[0].dtype),
            ],
        ),
        cost_estimate=pl.CostEstimate(
            flops=2 * slots * edge**3 * rank, bytes_accessed=2 * blocks.size, transcendentals=0
        ),
        input_output_aliases={3 + len(panels): 0, 4 + len(panels): 1},
        compiler_params=pltpu.CompilerParams(vmem_limit_bytes=48 << 20),
    )(table, live_counts, blocks, *panels, empty, empty + 0)


def on_device(blocks, coords, live_counts, mode2_factor, mode3_factor):
    x, core, z, y = (lax.axis_index(axis) for axis in PLACES)
    n_ja, n_ka = lax.axis_size(("x", "core")), lax.axis_size(("z", "y"))
    table = jnp.stack(
        [
            coords[:, 0],
            lax.rem(coords[:, 1], n_ka) ^ (z * lax.axis_size("y") + y),
            lax.rem(coords[:, 2], n_ja) ^ (x * CORES + core),
            jnp.broadcast_to(core, coords.shape[:1]),
        ],
        axis=1,
    )
    mode2_pieces = gather_pieces(mode2_factor, "z", "y")
    mode3_pieces = gather_pieces(mode3_factor, "x", "core")
    mode2_pieces[0] = pltpu.with_memory_space_constraint(mode2_factor, pltpu.HBM)
    mode3_pieces[0] = pltpu.with_memory_space_constraint(mode3_factor, pltpu.HBM)
    kept, sent = products(blocks, table, live_counts, mode2_pieces, mode3_pieces)
    received = exchange(sent, "core", 1)
    arrived = lax.all_to_all(kept + received, CHIPS, 0, 0, tiled=True)
    return arrived.sum(axis=0)


def solution(mesh):
    n_ja, n_ka = mesh.devices.shape
    near = 1
    while near * near * 4 <= n_ka:
        near *= 2
    places = Mesh(mesh.devices.reshape(n_ja // CORES, CORES, n_ka // near, near), PLACES)
    placed = (
        P(PLACES, None, None, None),
        P(PLACES, None),
        P(PLACES),
        P(PLACES, None),
        P(("z", "y", "x", "core"), None),
    )
    return jax.shard_map(
        on_device, mesh=places, in_specs=placed, out_specs=P(PLACES, None), check_vma=False
    )
```

```python
import functools

import jax
import jax.numpy as jnp
from jax import lax
from jax.experimental import pallas as pl
from jax.experimental.pallas import tpu as pltpu
from jax.sharding import Mesh
from jax.sharding import PartitionSpec as P


IROWS_DEV = 16
CORES = 2
STEP_ROWS = 64
PLACES = ("x", "core", "z", "y")
CHIPS = ("x", "z", "y")


def exchange(value, axis, code):
    size = lax.axis_size(axis)
    return lax.ppermute(value, axis, [(i, i ^ code) for i in range(size)])


def gather_pieces(own, far, near):
    far_size, near_size = lax.axis_size(far), lax.axis_size(near)
    pieces = {(0, 0): own}

    def fetch(code, source, axis, step):
        pieces[code] = exchange(pieces[source], axis, step)

    for far_code in range(far_size):
        low = far_code & -far_code
        rest = far_code ^ low
        if low and not rest:
            fetch((far_code, 0), (0, 0), far, far_code)
        elif low:
            fetch((far_code, 0), (rest, 0), far, low)
        for near_code in range(1, near_size):
            if rest:
                fetch((far_code, near_code), (low, near_code), far, rest)
            else:
                fetch((far_code, near_code), (far_code, 0), near, near_code)
    return [pieces[code] for code in sorted(pieces)]


def block_of(blocks_ref, index, steps):
    rows = pl.ds(index % steps * STEP_ROWS, STEP_ROWS)
    return blocks_ref.at[index // steps, rows]


def fetch_kernel(blocks_ref, mode2_ref, mode3_ref, *refs):
    cubes_ref, own2_ref, own3_ref, kept_ref, sent_ref, sems = refs
    copies = [
        pltpu.make_async_copy(source, target, sems.at[order])
        for order, (source, target) in enumerate(
            (
                (block_of(blocks_ref, 0, 1), cubes_ref.at[0]),
                (mode2_ref, own2_ref),
                (mode3_ref, own3_ref),
            )
        )
    ]
    for copy in copies:
        copy.start()
    kept_ref[...] = jnp.zeros_like(kept_ref)
    sent_ref[...] = jnp.zeros_like(sent_ref)
    for copy in copies:
        copy.wait()


def fetch_local(blocks, mode2_own, mode3_own, half_shape):
    edge = blocks.shape[1]
    in_hbm = pl.BlockSpec(memory_space=pl.ANY)
    in_place = pl.BlockSpec(memory_space=pltpu.VMEM)
    return pl.pallas_call(
        fetch_kernel,
        out_shape=[
            jax.ShapeDtypeStruct((2, STEP_ROWS, edge, edge), blocks.dtype),
            jax.ShapeDtypeStruct(mode2_own.shape, mode2_own.dtype),
            jax.ShapeDtypeStruct(mode3_own.shape, mode3_own.dtype),
            jax.ShapeDtypeStruct(half_shape, jnp.float32),
            jax.ShapeDtypeStruct(half_shape, jnp.float32),
        ],
        in_specs=[in_hbm] * 3,
        out_specs=[in_place] * 5,
        scratch_shapes=[pltpu.SemaphoreType.DMA((3,))],
        cost_estimate=pl.CostEstimate(flops=0, bytes_accessed=4 << 20, transcendentals=0),
        compiler_params=pltpu.CompilerParams(vmem_limit_bytes=2 << 20),
    )(blocks, mode2_own, mode3_own)


def product_kernel(n_ja, n_ka, steps, table, live, blocks_ref, *refs):
    mode2_refs, mode3_refs = refs[:n_ka], refs[n_ka : n_ka + n_ja]
    cubes_ref, kept_ref, sent_ref, mode2, mode3, sems = refs[n_ka + n_ja + 3 :]
    index = pl.program_id(0)
    slot, step = index // steps, index % steps
    edge, rank = mode2.shape
    last = live[0] * steps - 1

    def cubes_copy(at):
        side = at % 2
        return pltpu.make_async_copy(
            block_of(blocks_ref, at, steps), cubes_ref.at[side], sems.at[side]
        )

    @pl.when(index < last)
    def _():
        cubes_copy(index + 1).start()

    @pl.when(index <= last)
    def _():
        @pl.when(step == 0)
        def _():
            for code, ref in enumerate(mode2_refs):

                @pl.when(table[slot, 1] == code)
                def _(ref=ref):
                    mode2[...] = ref[...].astype(jnp.float32)

            for code, ref in enumerate(mode3_refs):

                @pl.when(table[slot, 2] == code)
                def _(ref=ref):
                    mode3[...] = ref[...]

        @pl.when(index > 0)
        def _():
            cubes_copy(index).wait()

        cube = cubes_ref[index % 2].reshape(STEP_ROWS * edge, edge)
        part = jnp.dot(cube, mode3[...], preferred_element_type=jnp.float32)
        part = (part.reshape(STEP_ROWS, edge, rank) * mode2[...][None]).sum(axis=1)
        first = (table[slot, 0] * edge + step * STEP_ROWS) // IROWS_DEV
        column = first // n_ka
        chip = column // CORES * n_ka + first % n_ka

        def add_to(ref):
            for piece in range(STEP_ROWS // IROWS_DEV):
                ref[chip + piece] += part[piece * IROWS_DEV : (piece + 1) * IROWS_DEV]

        pl.when(column % CORES == table[slot, 3])(functools.partial(add_to, kept_ref))
        pl.when(column % CORES != table[slot, 3])(functools.partial(add_to, sent_ref))


def products(blocks, table, live_counts, mode2_pieces, mode3_pieces, buffers):
    slots, edge = blocks.shape[:2]
    rank = mode2_pieces[0].shape[1]
    n_ka, n_ja = len(mode2_pieces), len(mode3_pieces)
    steps = edge // STEP_ROWS
    in_hbm = pl.BlockSpec(memory_space=pl.ANY)
    in_place = pl.BlockSpec(memory_space=pltpu.VMEM)
    panels = mode2_pieces + mode3_pieces
    _, kept, sent = pl.pallas_call(
        functools.partial(product_kernel, n_ja, n_ka, steps),
        out_shape=[jax.ShapeDtypeStruct(buffer.shape, buffer.dtype) for buffer in buffers],
        grid_spec=pltpu.PrefetchScalarGridSpec(
            num_scalar_prefetch=2,
            grid=(slots * steps,),
            in_specs=[in_hbm] + [in_place] * (len(panels) + len(buffers)),
            out_specs=[in_place] * len(buffers),
            scratch_shapes=[
                pltpu.VMEM((edge, rank), jnp.float32),
                pltpu.VMEM((edge, rank), mode3_pieces[0].dtype),
                pltpu.SemaphoreType.DMA((2,)),
            ],
        ),
        cost_estimate=pl.CostEstimate(
            flops=2 * slots * edge**3 * rank, bytes_accessed=2 * blocks.size, transcendentals=0
        ),
        input_output_aliases={3 + len(panels) + order: order for order in range(len(buffers))},
        compiler_params=pltpu.CompilerParams(vmem_limit_bytes=40 << 20),
    )(table, live_counts, blocks, *panels, *buffers)
    return kept, sent


def on_device(blocks, coords, live_counts, mode2_factor, mode3_factor):
    x, core, z, y = (lax.axis_index(axis) for axis in PLACES)
    n_ja, n_ka = lax.axis_size(("x", "core")), lax.axis_size(("z", "y"))
    table = jnp.stack(
        [
            coords[:, 0],
            lax.rem(coords[:, 1], n_ka) ^ (z * lax.axis_size("y") + y),
            lax.rem(coords[:, 2], n_ja) ^ (x * CORES + core),
            jnp.broadcast_to(core, coords.shape[:1]),
        ],
        axis=1,
    )
    mode2_pieces = gather_pieces(mode2_factor, "z", "y")
    mode3_pieces = gather_pieces(mode3_factor, "x", "core")
    blocks = pltpu.with_memory_space_constraint(blocks, pltpu.HBM)
    half_shape = (n_ja * n_ka // CORES, IROWS_DEV, mode2_factor.shape[1])
    cubes, mode2_pieces[0], mode3_pieces[0], kept, sent = fetch_local(
        blocks,
        pltpu.with_memory_space_constraint(mode2_factor, pltpu.HBM),
        pltpu.with_memory_space_constraint(mode3_factor, pltpu.HBM),
        half_shape,
    )
    kept, sent = products(
        blocks, table, live_counts, mode2_pieces, mode3_pieces, (cubes, kept, sent)
    )
    received = exchange(sent, "core", 1)
    arrived = lax.all_to_all(kept + received, CHIPS, 0, 0, tiled=True)
    return arrived.sum(axis=0)


def solution(mesh):
    n_ja, n_ka = mesh.devices.shape
    near = 1
    while near * near * 4 <= n_ka:
        near *= 2
    places = Mesh(mesh.devices.reshape(n_ja // CORES, CORES, n_ka // near, near), PLACES)
    placed = (
        P(PLACES, None, None, None),
        P(PLACES, None),
        P(PLACES),
        P(PLACES, None),
        P(("z", "y", "x", "core"), None),
    )
    return jax.shard_map(
        on_device, mesh=places, in_specs=placed, out_specs=P(PLACES, None), check_vma=False
    )
```

```python
import functools

import jax
import jax.numpy as jnp
from jax import lax
from jax.experimental import pallas as pl
from jax.experimental.pallas import tpu as pltpu
from jax.sharding import Mesh
from jax.sharding import PartitionSpec as P


IROWS_DEV = 16
CORES = 2
STEP_ROWS = 64
LANES = 128
SUBLANES = 8
WIRE = jnp.float16
WIRE_EXPONENT = 14.0
LEAST_EXPONENT = -100.0
LEAST = 1e-37
PLACES = ("x", "core", "z", "y")
CHIPS = ("x", "z", "y")


def exchange(value, axis, code):
    size = lax.axis_size(axis)
    return lax.ppermute(value, axis, [(i, i ^ code) for i in range(size)])


def gather_pieces(own, far, near):
    far_size, near_size = lax.axis_size(far), lax.axis_size(near)
    pieces = {(0, 0): own}

    def fetch(code, source, axis, step):
        pieces[code] = exchange(pieces[source], axis, step)

    for far_code in range(far_size):
        low = far_code & -far_code
        rest = far_code ^ low
        if low and not rest:
            fetch((far_code, 0), (0, 0), far, far_code)
        elif low:
            fetch((far_code, 0), (rest, 0), far, low)
        for near_code in range(1, near_size):
            if rest:
                fetch((far_code, near_code), (low, near_code), far, rest)
            else:
                fetch((far_code, near_code), (far_code, 0), near, near_code)
    return [pieces[code] for code in sorted(pieces)]


def block_of(blocks_ref, index, steps):
    rows = pl.ds(index % steps * STEP_ROWS, STEP_ROWS)
    return blocks_ref.at[index // steps, rows]


def fetch_kernel(blocks_ref, mode2_ref, mode3_ref, *refs):
    cubes_ref, own2_ref, own3_ref, kept_ref, sent_ref, sems = refs
    copies = [
        pltpu.make_async_copy(source, target, sems.at[order])
        for order, (source, target) in enumerate(
            (
                (block_of(blocks_ref, 0, 1), cubes_ref.at[0]),
                (mode2_ref, own2_ref),
                (mode3_ref, own3_ref),
            )
        )
    ]
    for copy in copies:
        copy.start()
    kept_ref[...] = jnp.zeros_like(kept_ref)
    sent_ref[...] = jnp.zeros_like(sent_ref)
    for copy in copies:
        copy.wait()


def fetch_local(blocks, mode2_own, mode3_own, half_shape):
    edge = blocks.shape[1]
    in_hbm = pl.BlockSpec(memory_space=pl.ANY)
    in_place = pl.BlockSpec(memory_space=pltpu.VMEM)
    return pl.pallas_call(
        fetch_kernel,
        out_shape=[
            jax.ShapeDtypeStruct((2, STEP_ROWS, edge, edge), blocks.dtype),
            jax.ShapeDtypeStruct(mode2_own.shape, mode2_own.dtype),
            jax.ShapeDtypeStruct(mode3_own.shape, mode3_own.dtype),
            jax.ShapeDtypeStruct(half_shape, jnp.float32),
            jax.ShapeDtypeStruct(half_shape, jnp.float32),
        ],
        in_specs=[in_hbm] * 3,
        out_specs=[in_place] * 5,
        scratch_shapes=[pltpu.SemaphoreType.DMA((3,))],
        cost_estimate=pl.CostEstimate(flops=0, bytes_accessed=4 << 20, transcendentals=0),
        compiler_params=pltpu.CompilerParams(vmem_limit_bytes=2 << 20),
    )(blocks, mode2_own, mode3_own)


def product_kernel(n_ja, n_ka, steps, table, live, blocks_ref, *refs):
    mode2_refs, mode3_refs = refs[:n_ka], refs[n_ka : n_ka + n_ja]
    cubes_ref, kept_ref, sent_ref, mode2, mode3, sems = refs[n_ka + n_ja + 3 :]
    index = pl.program_id(0)
    slot, step = index // steps, index % steps
    edge, rank = mode2.shape
    last = live[0] * steps - 1

    def cubes_copy(at):
        side = at % 2
        return pltpu.make_async_copy(
            block_of(blocks_ref, at, steps), cubes_ref.at[side], sems.at[side]
        )

    @pl.when(index < last)
    def _():
        cubes_copy(index + 1).start()

    @pl.when(index <= last)
    def _():
        @pl.when(step == 0)
        def _():
            for code, ref in enumerate(mode2_refs):

                @pl.when(table[slot, 1] == code)
                def _(ref=ref):
                    mode2[...] = ref[...].astype(jnp.float32)

            for code, ref in enumerate(mode3_refs):

                @pl.when(table[slot, 2] == code)
                def _(ref=ref):
                    mode3[...] = ref[...]

        @pl.when(index > 0)
        def _():
            cubes_copy(index).wait()

        cube = cubes_ref[index % 2].reshape(STEP_ROWS * edge, edge)
        part = jnp.dot(cube, mode3[...], preferred_element_type=jnp.float32)
        part = (part.reshape(STEP_ROWS, edge, rank) * mode2[...][None]).sum(axis=1)
        first = (table[slot, 0] * edge + step * STEP_ROWS) // IROWS_DEV
        column = first // n_ka
        chip = column // CORES * n_ka + first % n_ka

        def add_to(ref):
            for piece in range(STEP_ROWS // IROWS_DEV):
                for tile in range(rank // LANES):
                    ref[chip + piece, tile * IROWS_DEV : (tile + 1) * IROWS_DEV] += part[
                        piece * IROWS_DEV : (piece + 1) * IROWS_DEV,
                        tile * LANES : (tile + 1) * LANES,
                    ]

        pl.when(column % CORES == table[slot, 3])(functools.partial(add_to, kept_ref))
        pl.when(column % CORES != table[slot, 3])(functools.partial(add_to, sent_ref))

    @pl.when(index == last)
    def _():
        for ref in (kept_ref, sent_ref):
            bounds_at = ref.shape[1] - SUBLANES
            most = jnp.abs(ref[:, :SUBLANES])
            for row in range(SUBLANES, bounds_at, SUBLANES):
                most = jnp.maximum(most, jnp.abs(ref[:, row : row + SUBLANES]))
            ref[:, bounds_at:] = most


def products(blocks, table, live_counts, mode2_pieces, mode3_pieces, buffers):
    slots, edge = blocks.shape[:2]
    rank = mode2_pieces[0].shape[1]
    n_ka, n_ja = len(mode2_pieces), len(mode3_pieces)
    steps = edge // STEP_ROWS
    in_hbm = pl.BlockSpec(memory_space=pl.ANY)
    in_place = pl.BlockSpec(memory_space=pltpu.VMEM)
    panels = mode2_pieces + mode3_pieces
    _, kept, sent = pl.pallas_call(
        functools.partial(product_kernel, n_ja, n_ka, steps),
        out_shape=[jax.ShapeDtypeStruct(buffer.shape, buffer.dtype) for buffer in buffers],
        grid_spec=pltpu.PrefetchScalarGridSpec(
            num_scalar_prefetch=2,
            grid=(slots * steps,),
            in_specs=[in_hbm] + [in_place] * (len(panels) + len(buffers)),
            out_specs=[in_place] * len(buffers),
            scratch_shapes=[
                pltpu.VMEM((edge, rank), jnp.float32),
                pltpu.VMEM((edge, rank), mode3_pieces[0].dtype),
                pltpu.SemaphoreType.DMA((2,)),
            ],
        ),
        cost_estimate=pl.CostEstimate(
            flops=2 * slots * edge**3 * rank, bytes_accessed=2 * blocks.size, transcendentals=0
        ),
        input_output_aliases={3 + len(panels) + order: order for order in range(len(buffers))},
        compiler_params=pltpu.CompilerParams(vmem_limit_bytes=40 << 20),
    )(table, live_counts, blocks, *panels, *buffers)
    return kept, sent


def pack_kernel(kept_ref, received_ref, out_ref):
    bounds_at = out_ref.shape[1] - SUBLANES
    bound = kept_ref[:, bounds_at:] + received_ref[:, bounds_at:]
    exponent = jnp.maximum(jnp.floor(jnp.log2(jnp.maximum(bound, LEAST))), LEAST_EXPONENT)
    scale = jnp.exp2(WIRE_EXPONENT - exponent)
    for row in range(0, bounds_at, SUBLANES):
        rows = slice(row, row + SUBLANES)
        out_ref[:, rows] = (kept_ref[:, rows] + received_ref[:, rows]) * scale
    out_ref[:, bounds_at:] = exponent


def sum_kernel(arrived_ref, out_ref):
    bounds_at = arrived_ref.shape[1] - SUBLANES
    scale = jnp.exp2(arrived_ref[:, bounds_at:] - WIRE_EXPONENT)
    for row in range(0, bounds_at, SUBLANES):
        tile, place = divmod(row, IROWS_DEV)
        total = (arrived_ref[:, row : row + SUBLANES] * scale).sum(axis=0)
        out_ref[place : place + SUBLANES, tile * LANES : (tile + 1) * LANES] = total


def small_call(kernel, out_shape):
    return pl.pallas_call(
        kernel,
        out_shape=jax.ShapeDtypeStruct(out_shape, jnp.float32),
        compiler_params=pltpu.CompilerParams(vmem_limit_bytes=16 << 20),
    )


def on_device(blocks, coords, live_counts, mode2_factor, mode3_factor):
    x, core, z, y = (lax.axis_index(axis) for axis in PLACES)
    n_ja, n_ka = lax.axis_size(("x", "core")), lax.axis_size(("z", "y"))
    table = jnp.stack(
        [
            coords[:, 0],
            lax.rem(coords[:, 1], n_ka) ^ (z * lax.axis_size("y") + y),
            lax.rem(coords[:, 2], n_ja) ^ (x * CORES + core),
            jnp.broadcast_to(core, coords.shape[:1]),
        ],
        axis=1,
    )
    mode2_pieces = gather_pieces(mode2_factor, "z", "y")
    mode3_pieces = gather_pieces(mode3_factor, "x", "core")
    blocks = pltpu.with_memory_space_constraint(blocks, pltpu.HBM)
    rank = mode2_factor.shape[1]
    half_shape = (n_ja * n_ka // CORES, rank // LANES * IROWS_DEV + SUBLANES, LANES)
    cubes, mode2_pieces[0], mode3_pieces[0], kept, sent = fetch_local(
        blocks,
        pltpu.with_memory_space_constraint(mode2_factor, pltpu.HBM),
        pltpu.with_memory_space_constraint(mode3_factor, pltpu.HBM),
        half_shape,
    )
    kept, sent = products(
        blocks, table, live_counts, mode2_pieces, mode3_pieces, (cubes, kept, sent)
    )
    received = exchange(sent, "core", 1)
    packed = small_call(pack_kernel, half_shape)(kept, received).astype(WIRE)
    arrived = lax.all_to_all(packed, CHIPS, 0, 0, tiled=True).astype(jnp.float32)
    return small_call(sum_kernel, (IROWS_DEV, rank))(arrived)


def solution(mesh):
    n_ja, n_ka = mesh.devices.shape
    near = 1
    while near * near * 4 <= n_ka:
        near *= 2
    places = Mesh(mesh.devices.reshape(n_ja // CORES, CORES, n_ka // near, near), PLACES)
    placed = (
        P(PLACES, None, None, None),
        P(PLACES, None),
        P(PLACES),
        P(PLACES, None),
        P(("z", "y", "x", "core"), None),
    )
    return jax.shard_map(
        on_device, mesh=places, in_specs=placed, out_specs=P(PLACES, None), check_vma=False
    )
```

```python
import functools

import jax
import jax.numpy as jnp
from jax import lax
from jax.experimental import pallas as pl
from jax.experimental.pallas import tpu as pltpu
from jax.sharding import Mesh
from jax.sharding import PartitionSpec as P


IROWS_DEV = 16
CORES = 2
STEP_ROWS = 64
LANES = 128
SUBLANES = 8
WIRE = jnp.float16
WIRE_EXPONENT = 14.0
LEAST_EXPONENT = -100.0
LEAST = 1e-37
PLACES = ("x", "core", "z", "y")
CHIPS = ("x", "z", "y")


def exchange(value, axis, code):
    size = lax.axis_size(axis)
    return lax.ppermute(value, axis, [(i, i ^ code) for i in range(size)])


def gather_pieces(own, far, near):
    far_size, near_size = lax.axis_size(far), lax.axis_size(near)
    pieces = {(0, 0): own}

    def fetch(code, source, axis, step):
        pieces[code] = exchange(pieces[source], axis, step)

    for far_code in range(far_size):
        low = far_code & -far_code
        rest = far_code ^ low
        if low and not rest:
            fetch((far_code, 0), (0, 0), far, far_code)
        elif low:
            fetch((far_code, 0), (rest, 0), far, low)
        for near_code in range(1, near_size):
            if rest:
                fetch((far_code, near_code), (low, near_code), far, rest)
            else:
                fetch((far_code, near_code), (far_code, 0), near, near_code)
    return [pieces[code] for code in sorted(pieces)]


def is_late(far_code, near_code):
    return far_code >= 2 and (near_code > 0 or far_code & (far_code - 1) > 0)


def early_slot(table, live, early_codes):
    slots = table.shape[0]
    early = jnp.int32(slots)
    for slot in reversed(range(slots)):
        there = functools.reduce(jnp.logical_or, [table[slot, 1] == code for code in early_codes])
        early = jnp.where(there & (slot < live[0]), slot, early)
    found = early < slots
    return jnp.where(found, early, 0), found.astype(jnp.int32)


def slot_at(turn, early):
    return jnp.where(turn == 0, early, jnp.where(turn <= early, turn - 1, turn))


def block_of(blocks_ref, slot, step):
    rows = pl.ds(step * STEP_ROWS, STEP_ROWS)
    return blocks_ref.at[slot, rows]


def fetch_kernel(early_codes, table, live, blocks_ref, mode2_ref, mode3_ref, *refs):
    cubes_ref, own2_ref, own3_ref, kept_ref, sent_ref, sems = refs
    early, _ = early_slot(table, live, early_codes)
    copies = [
        pltpu.make_async_copy(source, target, sems.at[order])
        for order, (source, target) in enumerate(
            (
                (block_of(blocks_ref, early, 0), cubes_ref.at[0]),
                (mode2_ref, own2_ref),
                (mode3_ref, own3_ref),
            )
        )
    ]
    for copy in copies:
        copy.start()
    kept_ref[...] = jnp.zeros_like(kept_ref)
    sent_ref[...] = jnp.zeros_like(sent_ref)
    for copy in copies:
        copy.wait()


def fetch_local(early_codes, table, live_counts, blocks, mode2_own, mode3_own, half_shape):
    edge = blocks.shape[1]
    in_hbm = pl.BlockSpec(memory_space=pl.ANY)
    in_place = pl.BlockSpec(memory_space=pltpu.VMEM)
    return pl.pallas_call(
        functools.partial(fetch_kernel, early_codes),
        out_shape=[
            jax.ShapeDtypeStruct((2, STEP_ROWS, edge, edge), blocks.dtype),
            jax.ShapeDtypeStruct(mode2_own.shape, mode2_own.dtype),
            jax.ShapeDtypeStruct(mode3_own.shape, mode3_own.dtype),
            jax.ShapeDtypeStruct(half_shape, jnp.float32),
            jax.ShapeDtypeStruct(half_shape, jnp.float32),
        ],
        in_specs=[pl.BlockSpec(memory_space=pltpu.SMEM)] * 2 + [in_hbm] * 3,
        out_specs=[in_place] * 5,
        scratch_shapes=[pltpu.SemaphoreType.DMA((3,))],
        cost_estimate=pl.CostEstimate(flops=0, bytes_accessed=4 << 20, transcendentals=0),
        compiler_params=pltpu.CompilerParams(vmem_limit_bytes=2 << 20),
    )(table, live_counts, blocks, mode2_own, mode3_own)


def product_kernel(codes, n_ka, n_ja, steps, early_codes, is_early, table, live, *refs):
    blocks_ref, refs = refs[0], refs[1:]
    mode2_refs, mode3_refs = refs[: len(codes)], refs[len(codes) : len(codes) + n_ja]
    cubes_ref, kept_ref, sent_ref, mode2, mode3, sems = refs[len(codes) + n_ja + 3 :]
    edge, rank = mode2.shape
    early, found = early_slot(table, live, early_codes)
    total = live[0] * steps
    begin, end = (0, found * steps) if is_early else (found * steps, total)
    index = begin + pl.program_id(0)
    slot, step = slot_at(index // steps, early), index % steps

    def cubes_copy(at):
        side = at % 2
        source = block_of(blocks_ref, slot_at(at // steps, early), at % steps)
        return pltpu.make_async_copy(source, cubes_ref.at[side], sems.at[side])

    @pl.when((index < end) & (index + 1 < total))
    def _():
        cubes_copy(index + 1).start()

    @pl.when(index < end)
    def _():
        @pl.when(step == 0)
        def _():
            for code, ref in zip(codes, mode2_refs):

                @pl.when(table[slot, 1] == code)
                def _(ref=ref):
                    mode2[...] = ref[...].astype(jnp.float32)

            for code, ref in enumerate(mode3_refs):

                @pl.when(table[slot, 2] == code)
                def _(ref=ref):
                    mode3[...] = ref[...]

        @pl.when(index > begin)
        def _():
            cubes_copy(index).wait()

        cube = cubes_ref[index % 2].reshape(STEP_ROWS * edge, edge)
        part = jnp.dot(cube, mode3[...], preferred_element_type=jnp.float32)
        part = (part.reshape(STEP_ROWS, edge, rank) * mode2[...][None]).sum(axis=1)
        first = (table[slot, 0] * edge + step * STEP_ROWS) // IROWS_DEV
        column = first // n_ka
        chip = column // CORES * n_ka + first % n_ka

        def add_to(ref):
            for piece in range(STEP_ROWS // IROWS_DEV):
                for tile in range(rank // LANES):
                    ref[chip + piece, tile * IROWS_DEV : (tile + 1) * IROWS_DEV] += part[
                        piece * IROWS_DEV : (piece + 1) * IROWS_DEV,
                        tile * LANES : (tile + 1) * LANES,
                    ]

        pl.when(column % CORES == table[slot, 3])(functools.partial(add_to, kept_ref))
        pl.when(column % CORES != table[slot, 3])(functools.partial(add_to, sent_ref))

    if is_early:

        @pl.when((index == end - 1) & (index + 1 < total))
        def _():
            cubes_copy(index + 1).wait()

        return

    @pl.when(pl.program_id(0) == pl.num_programs(0) - 1)
    def _():
        for ref in (kept_ref, sent_ref):
            bounds_at = ref.shape[1] - SUBLANES
            most = jnp.abs(ref[:, :SUBLANES])
            for row in range(SUBLANES, bounds_at, SUBLANES):
                most = jnp.maximum(most, jnp.abs(ref[:, row : row + SUBLANES]))
            ref[:, bounds_at:] = most


def products(early_codes, is_early, blocks, table, live_counts, pieces, mode3_pieces, buffers):
    slots, edge = blocks.shape[:2]
    codes = early_codes if is_early else tuple(range(len(pieces)))
    panels = [pieces[code] for code in codes] + mode3_pieces
    rank = panels[0].shape[1]
    steps = edge // STEP_ROWS
    turns = 1 if is_early else slots
    in_hbm = pl.BlockSpec(memory_space=pl.ANY)
    in_place = pl.BlockSpec(memory_space=pltpu.VMEM)
    kernel = functools.partial(
        product_kernel, codes, len(pieces), len(mode3_pieces), steps, early_codes, is_early
    )
    return pl.pallas_call(
        kernel,
        out_shape=[jax.ShapeDtypeStruct(buffer.shape, buffer.dtype) for buffer in buffers],
        grid_spec=pltpu.PrefetchScalarGridSpec(
            num_scalar_prefetch=2,
            grid=(turns * steps,),
            in_specs=[in_hbm] + [in_place] * (len(panels) + len(buffers)),
            out_specs=[in_place] * len(buffers),
            scratch_shapes=[
                pltpu.VMEM((edge, rank), jnp.float32),
                pltpu.VMEM((edge, rank), mode3_pieces[0].dtype),
                pltpu.SemaphoreType.DMA((2,)),
            ],
        ),
        cost_estimate=pl.CostEstimate(
            flops=2 * turns * edge**3 * rank,
            bytes_accessed=2 * turns * edge**3,
            transcendentals=0,
        ),
        input_output_aliases={3 + len(panels) + order: order for order in range(len(buffers))},
        compiler_params=pltpu.CompilerParams(vmem_limit_bytes=40 << 20),
    )(table, live_counts, blocks, *panels, *buffers)


def pack_kernel(kept_ref, received_ref, out_ref):
    bounds_at = out_ref.shape[1] - SUBLANES
    bound = kept_ref[:, bounds_at:] + received_ref[:, bounds_at:]
    exponent = jnp.maximum(jnp.floor(jnp.log2(jnp.maximum(bound, LEAST))), LEAST_EXPONENT)
    scale = jnp.exp2(WIRE_EXPONENT - exponent)
    for row in range(0, bounds_at, SUBLANES):
        rows = slice(row, row + SUBLANES)
        out_ref[:, rows] = (kept_ref[:, rows] + received_ref[:, rows]) * scale
    out_ref[:, bounds_at:] = exponent


def sum_kernel(arrived_ref, out_ref):
    bounds_at = arrived_ref.shape[1] - SUBLANES
    scale = jnp.exp2(arrived_ref[:, bounds_at:] - WIRE_EXPONENT)
    for row in range(0, bounds_at, SUBLANES):
        tile, place = divmod(row, IROWS_DEV)
        total = (arrived_ref[:, row : row + SUBLANES] * scale).sum(axis=0)
        out_ref[place : place + SUBLANES, tile * LANES : (tile + 1) * LANES] = total


def small_call(kernel, out_shape):
    return pl.pallas_call(
        kernel,
        out_shape=jax.ShapeDtypeStruct(out_shape, jnp.float32),
        compiler_params=pltpu.CompilerParams(vmem_limit_bytes=16 << 20),
    )


def on_device(blocks, coords, live_counts, mode2_factor, mode3_factor):
    x, core, z, y = (lax.axis_index(axis) for axis in PLACES)
    n_ja, n_ka = lax.axis_size(("x", "core")), lax.axis_size(("z", "y"))
    table = jnp.stack(
        [
            coords[:, 0],
            lax.rem(coords[:, 1], n_ka) ^ (z * lax.axis_size("y") + y),
            lax.rem(coords[:, 2], n_ja) ^ (x * CORES + core),
            jnp.broadcast_to(core, coords.shape[:1]),
        ],
        axis=1,
    )
    mode2_pieces = gather_pieces(mode2_factor, "z", "y")
    mode3_pieces = gather_pieces(mode3_factor, "x", "core")
    blocks = pltpu.with_memory_space_constraint(blocks, pltpu.HBM)
    rank = mode2_factor.shape[1]
    half_shape = (n_ja * n_ka // CORES, rank // LANES * IROWS_DEV + SUBLANES, LANES)
    near_size = lax.axis_size("y")
    early_codes = tuple(code for code in range(n_ka) if not is_late(*divmod(code, near_size)))
    cubes, mode2_pieces[0], mode3_pieces[0], kept, sent = fetch_local(
        early_codes,
        table,
        live_counts,
        blocks,
        pltpu.with_memory_space_constraint(mode2_factor, pltpu.HBM),
        pltpu.with_memory_space_constraint(mode3_factor, pltpu.HBM),
        half_shape,
    )
    product = functools.partial(products, early_codes)
    args = blocks, table, live_counts, mode2_pieces, mode3_pieces
    buffers = product(True, *args, (cubes, kept, sent))
    _, kept, sent = product(False, *args, buffers)
    received = exchange(sent, "core", 1)
    packed = small_call(pack_kernel, half_shape)(kept, received).astype(WIRE)
    arrived = lax.all_to_all(packed, CHIPS, 0, 0, tiled=True).astype(jnp.float32)
    return small_call(sum_kernel, (IROWS_DEV, rank))(arrived)


def solution(mesh):
    n_ja, n_ka = mesh.devices.shape
    near = 1
    while near * near * 4 <= n_ka:
        near *= 2
    places = Mesh(mesh.devices.reshape(n_ja // CORES, CORES, n_ka // near, near), PLACES)
    placed = (
        P(PLACES, None, None, None),
        P(PLACES, None),
        P(PLACES),
        P(PLACES, None),
        P(("z", "y", "x", "core"), None),
    )
    return jax.shard_map(
        on_device, mesh=places, in_specs=placed, out_specs=P(PLACES, None), check_vma=False
    )
```

```python
import functools

import jax
import jax.numpy as jnp
from jax import lax
from jax.experimental import pallas as pl
from jax.experimental.pallas import tpu as pltpu
from jax.sharding import Mesh
from jax.sharding import PartitionSpec as P


IROWS_DEV = 16
CORES = 2
STEP_ROWS = 64
LANES = 128
SUBLANES = 8
WIRE = jnp.float16
WIRE_EXPONENT = 14.0
LEAST_EXPONENT = -100.0
LEAST = 1e-37
PLACES = ("x", "core", "z", "y")
CHIPS = ("x", "z", "y")


def exchange(value, axis, code):
    size = lax.axis_size(axis)
    return lax.ppermute(value, axis, [(i, i ^ code) for i in range(size)])


def gather_pieces(own, far, near):
    far_size, near_size = lax.axis_size(far), lax.axis_size(near)
    pieces = {(0, 0): own}

    def fetch(code, source, axis, step):
        pieces[code] = exchange(pieces[source], axis, step)

    for far_code in range(far_size):
        low = far_code & -far_code
        rest = far_code ^ low
        if low and not rest:
            fetch((far_code, 0), (0, 0), far, far_code)
        elif low:
            fetch((far_code, 0), (rest, 0), far, low)
        for near_code in range(1, near_size):
            if rest:
                fetch((far_code, near_code), (low, near_code), far, rest)
            else:
                fetch((far_code, near_code), (far_code, 0), near, near_code)
    return [pieces[code] for code in sorted(pieces)]


def is_late(far_code, near_code):
    return far_code >= 2 and (near_code > 0 or far_code & (far_code - 1) > 0)


def early_slot(table, live, early_codes):
    slots = table.shape[0]
    early = jnp.int32(slots)
    for slot in reversed(range(slots)):
        there = functools.reduce(jnp.logical_or, [table[slot, 1] == code for code in early_codes])
        early = jnp.where(there & (slot < live[0]), slot, early)
    found = early < slots
    return jnp.where(found, early, 0), found.astype(jnp.int32)


def slot_at(turn, early):
    return jnp.where(turn == 0, early, jnp.where(turn <= early, turn - 1, turn))


def block_of(blocks_ref, slot, step):
    rows = pl.ds(step * STEP_ROWS, STEP_ROWS)
    return blocks_ref.at[slot, rows]


def fetch_kernel(early_codes, table, live, blocks_ref, mode2_ref, mode3_ref, *refs):
    cubes_ref, own2_ref, own3_ref, kept_ref, sent_ref, sems = refs
    early, _ = early_slot(table, live, early_codes)
    copies = [
        pltpu.make_async_copy(source, target, sems.at[order])
        for order, (source, target) in enumerate(
            (
                (block_of(blocks_ref, early, 0), cubes_ref.at[0]),
                (mode2_ref, own2_ref),
                (mode3_ref, own3_ref),
            )
        )
    ]
    for copy in copies:
        copy.start()
    kept_ref[...] = jnp.zeros_like(kept_ref)
    sent_ref[...] = jnp.zeros_like(sent_ref)
    for copy in copies:
        copy.wait()


def fetch_local(early_codes, table, live_counts, blocks, mode2_own, mode3_own, half_shape):
    edge = blocks.shape[1]
    in_hbm = pl.BlockSpec(memory_space=pl.ANY)
    in_place = pl.BlockSpec(memory_space=pltpu.VMEM)
    return pl.pallas_call(
        functools.partial(fetch_kernel, early_codes),
        out_shape=[
            jax.ShapeDtypeStruct((2, STEP_ROWS, edge, edge), blocks.dtype),
            jax.ShapeDtypeStruct(mode2_own.shape, mode2_own.dtype),
            jax.ShapeDtypeStruct(mode3_own.shape, mode3_own.dtype),
            jax.ShapeDtypeStruct(half_shape, jnp.float32),
            jax.ShapeDtypeStruct(half_shape, jnp.float32),
        ],
        in_specs=[pl.BlockSpec(memory_space=pltpu.SMEM)] * 2 + [in_hbm] * 3,
        out_specs=[in_place] * 5,
        scratch_shapes=[pltpu.SemaphoreType.DMA((3,))],
        cost_estimate=pl.CostEstimate(flops=0, bytes_accessed=4 << 20, transcendentals=0),
        compiler_params=pltpu.CompilerParams(vmem_limit_bytes=2 << 20),
    )(table, live_counts, blocks, mode2_own, mode3_own)


def product_kernel(codes, n_ka, n_ja, steps, early_codes, is_early, table, live, *refs):
    blocks_ref, refs = refs[0], refs[1:]
    mode2_refs, mode3_refs = refs[: len(codes)], refs[len(codes) : len(codes) + n_ja]
    cubes_ref, kept_ref, sent_ref, mode2, mode3, sems = refs[len(codes) + n_ja + 3 :]
    edge, rank = mode2.shape
    early, found = early_slot(table, live, early_codes)
    total = live[0] * steps
    begin, end = (0, found * steps) if is_early else (found * steps, total)

    def cubes_copy(at):
        side = at % 2
        source = block_of(blocks_ref, slot_at(at // steps, early), at % steps)
        return pltpu.make_async_copy(source, cubes_ref.at[side], sems.at[side])

    def multiply(index, carry):
        slot, step = slot_at(index // steps, early), index % steps

        @pl.when(index + 1 < total)
        def _():
            cubes_copy(index + 1).start()

        @pl.when(step == 0)
        def _():
            for code, ref in zip(codes, mode2_refs):

                @pl.when(table[slot, 1] == code)
                def _(ref=ref):
                    mode2[...] = ref[...].astype(jnp.float32)

            for code, ref in enumerate(mode3_refs):

                @pl.when(table[slot, 2] == code)
                def _(ref=ref):
                    mode3[...] = ref[...]

        @pl.when(index > begin)
        def _():
            cubes_copy(index).wait()

        cube = cubes_ref[index % 2].reshape(STEP_ROWS * edge, edge)
        part = jnp.dot(cube, mode3[...], preferred_element_type=jnp.float32)
        part = (part.reshape(STEP_ROWS, edge, rank) * mode2[...][None]).sum(axis=1)
        first = (table[slot, 0] * edge + step * STEP_ROWS) // IROWS_DEV
        column = first // n_ka
        chip = column // CORES * n_ka + first % n_ka

        def add_to(ref):
            for piece in range(STEP_ROWS // IROWS_DEV):
                for tile in range(rank // LANES):
                    ref[chip + piece, tile * IROWS_DEV : (tile + 1) * IROWS_DEV] += part[
                        piece * IROWS_DEV : (piece + 1) * IROWS_DEV,
                        tile * LANES : (tile + 1) * LANES,
                    ]

        pl.when(column % CORES == table[slot, 3])(functools.partial(add_to, kept_ref))
        pl.when(column % CORES != table[slot, 3])(functools.partial(add_to, sent_ref))
        return carry

    lax.fori_loop(begin, end, multiply, 0)
    if is_early:

        @pl.when((end > begin) & (end < total))
        def _():
            cubes_copy(end).wait()

        return

    for ref in (kept_ref, sent_ref):
        bounds_at = ref.shape[1] - SUBLANES
        most = jnp.abs(ref[:, :SUBLANES])
        for row in range(SUBLANES, bounds_at, SUBLANES):
            most = jnp.maximum(most, jnp.abs(ref[:, row : row + SUBLANES]))
        ref[:, bounds_at:] = most


def products(early_codes, is_early, blocks, table, live_counts, pieces, mode3_pieces, buffers):
    slots, edge = blocks.shape[:2]
    codes = early_codes if is_early else tuple(range(len(pieces)))
    in_smem = pl.BlockSpec(memory_space=pltpu.SMEM)
    panels = [pieces[code] for code in codes] + mode3_pieces
    rank = panels[0].shape[1]
    steps = edge // STEP_ROWS
    turns = 1 if is_early else slots
    in_hbm = pl.BlockSpec(memory_space=pl.ANY)
    in_place = pl.BlockSpec(memory_space=pltpu.VMEM)
    kernel = functools.partial(
        product_kernel, codes, len(pieces), len(mode3_pieces), steps, early_codes, is_early
    )
    return pl.pallas_call(
        kernel,
        out_shape=[jax.ShapeDtypeStruct(buffer.shape, buffer.dtype) for buffer in buffers],
        in_specs=[in_smem] * 2 + [in_hbm] + [in_place] * (len(panels) + len(buffers)),
        out_specs=[in_place] * len(buffers),
        scratch_shapes=[
            pltpu.VMEM((edge, rank), jnp.float32),
            pltpu.VMEM((edge, rank), mode3_pieces[0].dtype),
            pltpu.SemaphoreType.DMA((2,)),
        ],
        cost_estimate=pl.CostEstimate(
            flops=2 * turns * edge**3 * rank,
            bytes_accessed=2 * turns * edge**3,
            transcendentals=0,
        ),
        input_output_aliases={3 + len(panels) + order: order for order in range(len(buffers))},
        compiler_params=pltpu.CompilerParams(vmem_limit_bytes=40 << 20),
    )(table, live_counts, blocks, *panels, *buffers)


def pack_kernel(kept_ref, received_ref, out_ref):
    bounds_at = out_ref.shape[1] - SUBLANES
    bound = kept_ref[:, bounds_at:] + received_ref[:, bounds_at:]
    exponent = jnp.maximum(jnp.floor(jnp.log2(jnp.maximum(bound, LEAST))), LEAST_EXPONENT)
    scale = jnp.exp2(WIRE_EXPONENT - exponent)
    for row in range(0, bounds_at, SUBLANES):
        rows = slice(row, row + SUBLANES)
        out_ref[:, rows] = (kept_ref[:, rows] + received_ref[:, rows]) * scale
    out_ref[:, bounds_at:] = exponent


def sum_kernel(arrived_ref, out_ref):
    bounds_at = arrived_ref.shape[1] - SUBLANES
    scale = jnp.exp2(arrived_ref[:, bounds_at:] - WIRE_EXPONENT)
    for row in range(0, bounds_at, SUBLANES):
        tile, place = divmod(row, IROWS_DEV)
        total = (arrived_ref[:, row : row + SUBLANES] * scale).sum(axis=0)
        out_ref[place : place + SUBLANES, tile * LANES : (tile + 1) * LANES] = total


def small_call(kernel, out_shape):
    return pl.pallas_call(
        kernel,
        out_shape=jax.ShapeDtypeStruct(out_shape, jnp.float32),
        compiler_params=pltpu.CompilerParams(vmem_limit_bytes=16 << 20),
    )


def on_device(blocks, coords, live_counts, mode2_factor, mode3_factor):
    x, core, z, y = (lax.axis_index(axis) for axis in PLACES)
    n_ja, n_ka = lax.axis_size(("x", "core")), lax.axis_size(("z", "y"))
    table = jnp.stack(
        [
            coords[:, 0],
            lax.rem(coords[:, 1], n_ka) ^ (z * lax.axis_size("y") + y),
            lax.rem(coords[:, 2], n_ja) ^ (x * CORES + core),
            jnp.broadcast_to(core, coords.shape[:1]),
        ],
        axis=1,
    )
    mode2_pieces = gather_pieces(mode2_factor, "z", "y")
    mode3_pieces = gather_pieces(mode3_factor, "x", "core")
    blocks = pltpu.with_memory_space_constraint(blocks, pltpu.HBM)
    rank = mode2_factor.shape[1]
    half_shape = (n_ja * n_ka // CORES, rank // LANES * IROWS_DEV + SUBLANES, LANES)
    near_size = lax.axis_size("y")
    early_codes = tuple(code for code in range(n_ka) if not is_late(*divmod(code, near_size)))
    cubes, mode2_pieces[0], mode3_pieces[0], kept, sent = fetch_local(
        early_codes,
        table,
        live_counts,
        blocks,
        pltpu.with_memory_space_constraint(mode2_factor, pltpu.HBM),
        pltpu.with_memory_space_constraint(mode3_factor, pltpu.HBM),
        half_shape,
    )
    product = functools.partial(products, early_codes)
    args = blocks, table, live_counts, mode2_pieces, mode3_pieces
    buffers = product(True, *args, (cubes, kept, sent))
    _, kept, sent = product(False, *args, buffers)
    received = exchange(sent, "core", 1)
    packed = small_call(pack_kernel, half_shape)(kept, received).astype(WIRE)
    arrived = lax.all_to_all(packed, CHIPS, 0, 0, tiled=True).astype(jnp.float32)
    return small_call(sum_kernel, (IROWS_DEV, rank))(arrived)


def solution(mesh):
    n_ja, n_ka = mesh.devices.shape
    near = 1
    while near * near * 4 <= n_ka:
        near *= 2
    places = Mesh(mesh.devices.reshape(n_ja // CORES, CORES, n_ka // near, near), PLACES)
    placed = (
        P(PLACES, None, None, None),
        P(PLACES, None),
        P(PLACES),
        P(PLACES, None),
        P(("z", "y", "x", "core"), None),
    )
    return jax.shard_map(
        on_device, mesh=places, in_specs=placed, out_specs=P(PLACES, None), check_vma=False
    )
```

```python
import functools

import jax
import jax.numpy as jnp
from jax import lax
from jax.experimental import pallas as pl
from jax.experimental.pallas import tpu as pltpu
from jax.sharding import Mesh
from jax.sharding import PartitionSpec as P


IROWS_DEV = 16
CORES = 2
EARLY_ROWS = 64
LANES = 128
SUBLANES = 8
WIRE = jnp.float16
WIRE_EXPONENT = 14.0
LEAST_EXPONENT = -100.0
LEAST = 1e-37
PLACES = ("x", "core", "z", "y")
CHIPS = ("x", "z", "y")


def exchange(value, axis, code):
    size = lax.axis_size(axis)
    return lax.ppermute(value, axis, [(i, i ^ code) for i in range(size)])


def gather_pieces(own, far, near):
    far_size, near_size = lax.axis_size(far), lax.axis_size(near)
    pieces = {(0, 0): own}

    def fetch(code, source, axis, step):
        pieces[code] = exchange(pieces[source], axis, step)

    for far_code in range(far_size):
        low = far_code & -far_code
        rest = far_code ^ low
        if low and not rest:
            fetch((far_code, 0), (0, 0), far, far_code)
        elif low:
            fetch((far_code, 0), (rest, 0), far, low)
        for near_code in range(1, near_size):
            if rest:
                fetch((far_code, near_code), (low, near_code), far, rest)
            else:
                fetch((far_code, near_code), (far_code, 0), near, near_code)
    return [pieces[code] for code in sorted(pieces)]


def is_late(far_code, near_code):
    return far_code >= 2 and (near_code > 0 or far_code & (far_code - 1) > 0)


def early_slot(table, live, early_codes):
    slots = table.shape[0]
    early = jnp.int32(slots)
    for slot in reversed(range(slots)):
        there = functools.reduce(jnp.logical_or, [table[slot, 1] == code for code in early_codes])
        early = jnp.where(there & (slot < live[0]), slot, early)
    found = early < slots
    return jnp.where(found, early, 0), found.astype(jnp.int32)


def slot_at(turn, early):
    return jnp.where(turn == 0, early, jnp.where(turn <= early, turn - 1, turn))


def fetch_kernel(early_codes, table, live, blocks_ref, mode2_ref, mode3_ref, *refs):
    cubes_ref, own2_ref, own3_ref, kept_ref, sent_ref, sems = refs
    early, _ = early_slot(table, live, early_codes)
    first_rows = pl.ds(0, EARLY_ROWS)
    copies = [
        pltpu.make_async_copy(source, target, sems.at[order])
        for order, (source, target) in enumerate(
            (
                (blocks_ref.at[early, first_rows], cubes_ref.at[0, first_rows]),
                (mode2_ref, own2_ref),
                (mode3_ref, own3_ref),
            )
        )
    ]
    for copy in copies:
        copy.start()
    kept_ref[...] = jnp.zeros_like(kept_ref)
    sent_ref[...] = jnp.zeros_like(sent_ref)
    for copy in copies:
        copy.wait()


def fetch_local(early_codes, table, live_counts, blocks, mode2_own, mode3_own, half_shape):
    edge = blocks.shape[1]
    in_hbm = pl.BlockSpec(memory_space=pl.ANY)
    in_place = pl.BlockSpec(memory_space=pltpu.VMEM)
    return pl.pallas_call(
        functools.partial(fetch_kernel, early_codes),
        out_shape=[
            jax.ShapeDtypeStruct((2, edge, edge, edge), blocks.dtype),
            jax.ShapeDtypeStruct(mode2_own.shape, mode2_own.dtype),
            jax.ShapeDtypeStruct(mode3_own.shape, mode3_own.dtype),
            jax.ShapeDtypeStruct(half_shape, jnp.float32),
            jax.ShapeDtypeStruct(half_shape, jnp.float32),
        ],
        in_specs=[pl.BlockSpec(memory_space=pltpu.SMEM)] * 2 + [in_hbm] * 3,
        out_specs=[in_place] * 5,
        scratch_shapes=[pltpu.SemaphoreType.DMA((3,))],
        cost_estimate=pl.CostEstimate(flops=0, bytes_accessed=4 << 20, transcendentals=0),
        compiler_params=pltpu.CompilerParams(vmem_limit_bytes=2 << 20),
    )(table, live_counts, blocks, mode2_own, mode3_own)


def select(table, column, slot, codes, refs, target):
    for code, ref in zip(codes, refs):

        @pl.when(table[slot, column] == code)
        def _(ref=ref):
            target[...] = ref[...].astype(target.dtype)


def add_product(table, n_ka, slot, start, cube, mode2, mode3, kept_ref, sent_ref):
    rows, edge = cube.shape[:2]
    rank = mode3.shape[1]
    part = jnp.dot(
        cube.reshape(rows * edge, edge), mode3[...], preferred_element_type=jnp.float32
    )
    part = (part.reshape(rows, edge, rank) * mode2[...][None]).sum(axis=1)
    first = (table[slot, 0] * edge + start) // IROWS_DEV
    column = first // n_ka
    chip = column // CORES * n_ka + first % n_ka

    def add_to(ref):
        for piece in range(rows // IROWS_DEV):
            for tile in range(rank // LANES):
                ref[chip + piece, tile * IROWS_DEV : (tile + 1) * IROWS_DEV] += part[
                    piece * IROWS_DEV : (piece + 1) * IROWS_DEV,
                    tile * LANES : (tile + 1) * LANES,
                ]

    pl.when(column % CORES == table[slot, 3])(functools.partial(add_to, kept_ref))
    pl.when(column % CORES != table[slot, 3])(functools.partial(add_to, sent_ref))


def product_kernel(codes, n_ka, n_ja, early_codes, is_early, table, live, *refs):
    blocks_ref, refs = refs[0], refs[1:]
    mode2_refs, mode3_refs = refs[: len(codes)], refs[len(codes) : len(codes) + n_ja]
    cubes_ref, kept_ref, sent_ref, mode2, mode3, sems = refs[len(codes) + n_ja + 3 :]
    edge = mode2.shape[0]
    early, found = early_slot(table, live, early_codes)

    def slot_copy(turn):
        side = turn % 2
        return pltpu.make_async_copy(
            blocks_ref.at[slot_at(turn, early)], cubes_ref.at[side], sems.at[side]
        )

    def choose(slot):
        select(table, 1, slot, codes, mode2_refs, mode2)
        select(table, 2, slot, range(n_ja), mode3_refs, mode3)

    def add(slot, start, cube):
        add_product(table, n_ka, slot, start, cube, mode2, mode3, kept_ref, sent_ref)

    if is_early:

        later_rows = pl.ds(EARLY_ROWS, edge - EARLY_ROWS)
        rest = pltpu.make_async_copy(
            blocks_ref.at[early, later_rows], cubes_ref.at[0, later_rows], sems.at[0]
        )
        rest.start()

        @pl.when(found == 0)
        def _():
            rest.wait()

        @pl.when(found == 1)
        def _():
            choose(early)
            pl.when(live[0] > 1)(lambda: slot_copy(1).start())
            add(early, 0, cubes_ref[0, :EARLY_ROWS])
            rest.wait()
            for start in range(EARLY_ROWS, edge, EARLY_ROWS):
                add(early, start, cubes_ref[0, start : start + EARLY_ROWS])
            pl.when(live[0] > 1)(lambda: slot_copy(1).wait())

        return

    def multiply(turn, carry):
        slot = slot_at(turn, early)
        pl.when(turn > found)(lambda: slot_copy(turn).wait())
        pl.when(turn + 1 < live[0])(lambda: slot_copy(turn + 1).start())
        choose(slot)
        add(slot, 0, cubes_ref[turn % 2])
        return carry

    lax.fori_loop(found, live[0], multiply, 0)


def products(early_codes, is_early, blocks, table, live_counts, pieces, mode3_pieces, buffers):
    slots, edge = blocks.shape[:2]
    codes = early_codes if is_early else tuple(range(len(pieces)))
    in_smem = pl.BlockSpec(memory_space=pltpu.SMEM)
    panels = [pieces[code] for code in codes] + mode3_pieces
    rank = panels[0].shape[1]
    turns = 1 if is_early else slots
    in_hbm = pl.BlockSpec(memory_space=pl.ANY)
    in_place = pl.BlockSpec(memory_space=pltpu.VMEM)
    kernel = functools.partial(
        product_kernel, codes, len(pieces), len(mode3_pieces), early_codes, is_early
    )
    return pl.pallas_call(
        kernel,
        out_shape=[jax.ShapeDtypeStruct(buffer.shape, buffer.dtype) for buffer in buffers],
        in_specs=[in_smem] * 2 + [in_hbm] + [in_place] * (len(panels) + len(buffers)),
        out_specs=[in_place] * len(buffers),
        scratch_shapes=[
            pltpu.VMEM((edge, rank), jnp.float32),
            pltpu.VMEM((edge, rank), mode3_pieces[0].dtype),
            pltpu.SemaphoreType.DMA((2,)),
        ],
        cost_estimate=pl.CostEstimate(
            flops=2 * turns * edge**3 * rank,
            bytes_accessed=2 * turns * edge**3,
            transcendentals=0,
        ),
        input_output_aliases={3 + len(panels) + order: order for order in range(len(buffers))},
        compiler_params=pltpu.CompilerParams(vmem_limit_bytes=40 << 20),
    )(table, live_counts, blocks, *panels, *buffers)


def pack_kernel(kept_ref, received_ref, out_ref):
    bounds_at = kept_ref.shape[1]
    groups = range(0, bounds_at, SUBLANES)
    most = jnp.full((kept_ref.shape[0], SUBLANES, LANES), LEAST, jnp.float32)
    for row in groups:
        rows = slice(row, row + SUBLANES)
        total = kept_ref[:, rows] + received_ref[:, rows]
        out_ref[:, rows] = total
        most = jnp.maximum(most, jnp.abs(total))
    exponent = jnp.maximum(jnp.floor(jnp.log2(most)), LEAST_EXPONENT)
    scale = jnp.exp2(WIRE_EXPONENT - exponent)
    for row in groups:
        rows = slice(row, row + SUBLANES)
        out_ref[:, rows] = out_ref[:, rows] * scale
    out_ref[:, bounds_at:] = exponent


def sum_kernel(arrived_ref, out_ref):
    bounds_at = arrived_ref.shape[1] - SUBLANES
    scale = jnp.exp2(arrived_ref[:, bounds_at:] - WIRE_EXPONENT)
    for row in range(0, bounds_at, SUBLANES):
        tile, place = divmod(row, IROWS_DEV)
        total = (arrived_ref[:, row : row + SUBLANES] * scale).sum(axis=0)
        out_ref[place : place + SUBLANES, tile * LANES : (tile + 1) * LANES] = total


def small_call(kernel, out_shape):
    return pl.pallas_call(
        kernel,
        out_shape=jax.ShapeDtypeStruct(out_shape, jnp.float32),
        compiler_params=pltpu.CompilerParams(vmem_limit_bytes=16 << 20),
    )


def on_device(blocks, coords, live_counts, mode2_factor, mode3_factor):
    x, core, z, y = (lax.axis_index(axis) for axis in PLACES)
    n_ja, n_ka = lax.axis_size(("x", "core")), lax.axis_size(("z", "y"))
    table = jnp.stack(
        [
            coords[:, 0],
            lax.rem(coords[:, 1], n_ka) ^ (z * lax.axis_size("y") + y),
            lax.rem(coords[:, 2], n_ja) ^ (x * CORES + core),
            jnp.broadcast_to(core, coords.shape[:1]),
        ],
        axis=1,
    )
    mode2_pieces = gather_pieces(mode2_factor, "z", "y")
    mode3_pieces = gather_pieces(mode3_factor, "x", "core")
    blocks = pltpu.with_memory_space_constraint(blocks, pltpu.HBM)
    rank = mode2_factor.shape[1]
    half_shape = (n_ja * n_ka // CORES, rank // LANES * IROWS_DEV, LANES)
    near_size = lax.axis_size("y")
    early_codes = tuple(code for code in range(n_ka) if not is_late(*divmod(code, near_size)))
    cubes, mode2_pieces[0], mode3_pieces[0], kept, sent = fetch_local(
        early_codes,
        table,
        live_counts,
        blocks,
        pltpu.with_memory_space_constraint(mode2_factor, pltpu.HBM),
        pltpu.with_memory_space_constraint(mode3_factor, pltpu.HBM),
        half_shape,
    )
    product = functools.partial(products, early_codes)
    args = blocks, table, live_counts, mode2_pieces, mode3_pieces
    buffers = product(True, *args, (cubes, kept, sent))
    _, kept, sent = product(False, *args, buffers)
    received = exchange(sent, "core", 1)
    wire_shape = (half_shape[0], half_shape[1] + SUBLANES, LANES)
    packed = small_call(pack_kernel, wire_shape)(kept, received).astype(WIRE)
    arrived = lax.all_to_all(packed, CHIPS, 0, 0, tiled=True).astype(jnp.float32)
    return small_call(sum_kernel, (IROWS_DEV, rank))(arrived)


def solution(mesh):
    n_ja, n_ka = mesh.devices.shape
    near = 1
    while near * near * 4 <= n_ka:
        near *= 2
    places = Mesh(mesh.devices.reshape(n_ja // CORES, CORES, n_ka // near, near), PLACES)
    placed = (
        P(PLACES, None, None, None),
        P(PLACES, None),
        P(PLACES),
        P(PLACES, None),
        P(("z", "y", "x", "core"), None),
    )
    return jax.shard_map(
        on_device, mesh=places, in_specs=placed, out_specs=P(PLACES, None), check_vma=False
    )
```
